512 devices in a mesh: kern: 4 (over y), tile: 128 (over x, z, core).
Axes of the slice: x: 4, y: 4, z: 16, core: 2. Of those that a mesh axis runs over, the one named last changes fastest.
Arguments:
- diag_tiles: float32 [4, 128, 512, 512], P('kern', 'tile'), may hold values from -0.25 to 0.25
- left_factors: float32 [4, 128, 8, 80, 512], P('kern', 'tile'), may hold values from -0.25 to 0.25
- right_factors: float32 [4, 128, 12, 80, 512], P('kern', 'tile'), may hold values from -0.25 to 0.25
- tile_offsets: int32 [4, 128, 8], P('kern', 'tile'), may hold values from -6 to 6, as said below
- tile_ranks: int32 [4, 128, 8], P('kern', 'tile'), may hold values from 32 to 80
- mixing: float32 [64, 4, 4], replicated, may hold values from -3 to 3
- block_index: int32 [65536], P('tile'), may hold values from 0 to 63
- rhs_field: float32 [4, 65536, 128], P('kern', 'tile'), may hold values from -6 to 6
Outputs:
- product: float32 [4, 65536, 128], P('kern', 'tile')
The draws below stay inside these ranges and needn't reach their ends.
Inputs may be any that keep to these rules, and one draw needn't show every extreme that they name: `tile_offsets`: each row's 8 offsets are distinct and nonzero.
All inputs are finite; a program needn't handle non-finite values.
Results may differ from the reference program's by a relative error of at most 0.00007.
Values sent between devices are 32-bit elements; how exact they have to be, the bound alone decides.
A program may use at most 64 MiB of HBM per device.

```python
import jax
import jax.numpy as jnp
from jax import lax

LATENT_KERNELS = 4
B = 512
RMAX = 80
OFFDIAG_TILES = 8
REACH = 6
C = 128
NBLK = 64
TILE_ROWS = 128
N = 65536
RMIN = 32


def draw_tile_offsets(key, part):
    candidate_list = 2 * REACH
    rating_values = jax.random.randint(key, (LATENT_KERNELS, TILE_ROWS, candidate_list), 0, 2 ** 20) * 32 + jnp.arange(candidate_list, dtype=jnp.int32)
    extra_credit = jnp.zeros((LATENT_KERNELS, TILE_ROWS, candidate_list), jnp.int32).at[:, 0, 0].set(2 ** 26).at[:, TILE_ROWS - 1, candidate_list - 1].set(2 ** 26)
    sorted_order = jnp.argsort(rating_values - extra_credit, axis=-1)[..., :OFFDIAG_TILES]
    return jnp.where(sorted_order < REACH, sorted_order - REACH, sorted_order - REACH + 1).astype(jnp.int32)


def draw_tile_ranks(key, part):
    values = jax.random.randint(key, (LATENT_KERNELS, TILE_ROWS, OFFDIAG_TILES), RMIN, RMAX + 1)
    return values.at[:, 0, 0].set(RMAX).at[:, 0, 1].set(RMIN).astype(jnp.int32)


def draw_block_index(key, part):
    values = jax.random.randint(key, (N,), 0, NBLK)
    spread = jax.random.permutation(jax.random.fold_in(key, 7), NBLK)
    return values.at[:NBLK].set(spread).astype(jnp.int32)


def block_scale(key, shape, shards, least, top_value):
    def one(axis_at, parts):
        draws = jax.random.uniform(jax.random.fold_in(jax.random.fold_in(key, 6), axis_at), (parts,), jnp.float32, least / len(shards), top_value / len(shards))
        return jnp.repeat(jnp.exp(draws), shape[axis_at] // parts).reshape((-1,) + (1,) * (len(shape) - axis_at - 1))

    gain = one(*shards[0])
    for cut in shards[1:]:
        gain = gain * one(*cut)
    return gain


def centred(stream_key, shape, width, limit, cuts=(), kind=jnp.bfloat16):
    drawn = width * jax.random.normal(stream_key, shape, jnp.float32)
    if cuts:
        drawn = drawn * block_scale(stream_key, shape, cuts, -0.22, 0.18)
    return jnp.clip(drawn, -limit, limit).astype(kind)


def setup_inputs(seed: int = 0) -> dict:
    arg_keys = jax.random.split(jax.random.key(seed), 9)
    return {
        "diag_tiles": centred(arg_keys[0], (LATENT_KERNELS, TILE_ROWS, B, B), B ** -0.5, 0.25, ((0, 4), (1, 128)), jnp.float32),
        "left_factors": centred(arg_keys[1], (LATENT_KERNELS, TILE_ROWS, OFFDIAG_TILES, RMAX, B), (OFFDIAG_TILES * RMAX) ** -0.5, 0.25, ((0, 4), (1, 128)), jnp.float32),
        "right_factors": centred(arg_keys[2], (LATENT_KERNELS, TILE_ROWS, 2 * REACH, RMAX, B), B ** -0.5, 0.25, ((0, 4), (1, 128)), jnp.float32),
        "tile_offsets": draw_tile_offsets(jax.random.fold_in(arg_keys[8], 71), 0),
        "tile_ranks": draw_tile_ranks(jax.random.fold_in(arg_keys[8], 71), 0),
        "mixing": centred(arg_keys[5], (NBLK, LATENT_KERNELS, LATENT_KERNELS), 0.5, 3.0, (), jnp.float32),
        "block_index": draw_block_index(jax.random.fold_in(arg_keys[8], 71), 0),
        "rhs_field": centred(arg_keys[7], (LATENT_KERNELS, N, C), 1.0, 6.0, ((0, 4), (1, 128)), jnp.float32),
    }


highest = lax.Precision.HIGHEST


def apply_kernel(diag_group, left_group, right_group, offsets_group, ranks_group, columns):
    tiles_n = diag_group.shape[0]
    tile_width = diag_group.shape[1]
    blocks = columns.reshape(tiles_n, tile_width, -1)
    coeffs = jnp.einsum('tsqp,tpc->tsqc', right_group, blocks, precision=highest)
    source = (jnp.arange(tiles_n, dtype=jnp.int32)[:, None] + offsets_group) % tiles_n
    slot_pick = jnp.where(offsets_group < 0, offsets_group + REACH, offsets_group + REACH - 1)
    chosen = coeffs[source.astype(jnp.int32), slot_pick.astype(jnp.int32)]
    keeper = (jnp.arange(left_group.shape[2], dtype=jnp.int32)[None, None, :] < ranks_group[:, :, None]).astype(jnp.float32)
    chosen = chosen * keeper[..., None]
    result = jnp.einsum('tpr,trc->tpc', diag_group, blocks, precision=highest)
    result = result + jnp.einsum('tkqp,tkqc->tpc', left_group, chosen, precision=highest)
    return result.reshape(tiles_n * tile_width, -1)


def reference(diag_tiles, left_factors, right_factors, tile_offsets, tile_ranks, mixing, block_index, rhs_field):
    first = jnp.stack([apply_kernel(diag_tiles[group], left_factors[group], right_factors[group], tile_offsets[group], tile_ranks[group], rhs_field[group]) for group in range(LATENT_KERNELS)])
    per_location = mixing[block_index.astype(jnp.int32)]
    mixed = jnp.einsum('lab,blc->alc', per_location, first, precision=highest)
    return jnp.stack([apply_kernel(diag_tiles[group], left_factors[group], right_factors[group], tile_offsets[group], tile_ranks[group], mixed[group]) for group in range(LATENT_KERNELS)])
```

```python
import functools

import jax
import jax.numpy as jnp
from jax import lax
from jax.experimental import pallas as pl
from jax.experimental.pallas import tpu as pltpu
from jax.sharding import PartitionSpec as P

MESH = pl.DeviceIdType.MESH
REACH = 6
SLOTS = 2 * REACH
ORDER = tuple(slot for far in range(REACH, 0, -1) for slot in (REACH - far, REACH + far - 1))
GROUP = 3
GROUPS = SLOTS // GROUP


def offset_of(slot):
    return slot - REACH if slot < REACH else slot - REACH + 1


def split(value):
    high = value.astype(jnp.bfloat16)
    return high, (value - high.astype(jnp.float32)).astype(jnp.bfloat16)


def dot(a, b):
    return jnp.dot(a, b, preferred_element_type=jnp.float32)


def product(high, low, pair):
    width = pair.shape[1] // 2
    wide = dot(high, pair)
    return wide[:, :width] + wide[:, width:] + dot(low, pair[:, :width])


def kernel(
    tiles,
    kerns,
    diag_hbm,
    left_hbm,
    right_hbm,
    offsets_hbm,
    ranks_hbm,
    mixing_hbm,
    index_hbm,
    rhs_hbm,
    out_ref,
    column,
    diag_f32,
    left_f32,
    right_f32,
    offsets,
    ranks,
    mixing,
    index,
    diag_hi,
    diag_lo,
    right_hi,
    right_lo,
    left_hi,
    left_lo,
    pair,
    arrived_pair,
    coeffs,
    arrived,
    total,
    blend,
    gathered,
    mixed_out,
    second,
    load_sem,
    right_sem,
    send_sem,
    recv_sem,
    field_send,
    field_recv,
):
    me = lax.axis_index("tile")
    group = lax.axis_index("kern")
    rows, cols = column.shape
    rank_max = right_f32.shape[1]
    depth = arrived.shape[2]
    part = rows // kerns

    def tile_at(offset):
        return (group, lax.rem(me + offset + tiles, tiles))

    def kern_at(ahead):
        return (lax.rem(group + ahead, kerns), me)

    def part_rows(ahead):
        return pl.ds(pl.multiple_of(lax.rem(group + ahead, kerns) * part, part), part)

    barrier = pltpu.get_barrier_semaphore()
    for slot in ORDER:
        pl.semaphore_signal(barrier, inc=1, device_id=tile_at(offset_of(slot)), device_id_type=MESH)
    for ahead in range(1, kerns):
        pl.semaphore_signal(barrier, inc=1, device_id=kern_at(ahead), device_id_type=MESH)

    load_rhs = pltpu.make_async_copy(rhs_hbm.at[0], column, load_sem.at[0])
    load_rhs.start()
    load_right = []
    for place, slot in enumerate(ORDER):
        copy = pltpu.make_async_copy(right_hbm.at[0, 0, slot], right_f32.at[place], right_sem.at[place])
        copy.start()
        load_right.append(copy)
    load_left = pltpu.make_async_copy(left_hbm.at[0, 0], left_f32, load_sem.at[1])
    load_diag = pltpu.make_async_copy(diag_hbm.at[0, 0], diag_f32, load_sem.at[2])
    load_offsets = pltpu.make_async_copy(offsets_hbm, offsets, load_sem.at[3])
    load_ranks = pltpu.make_async_copy(ranks_hbm, ranks, load_sem.at[4])
    load_mixing = pltpu.make_async_copy(mixing_hbm, mixing, load_sem.at[5])
    load_index = pltpu.make_async_copy(index_hbm, index, load_sem.at[6])
    for copy in (load_offsets, load_ranks, load_left, load_diag, load_mixing, load_index):
        copy.start()

    def send_coeffs(turn, place):
        copy = pltpu.make_async_remote_copy(
            src_ref=coeffs.at[turn, place],
            dst_ref=arrived.at[turn, place // GROUP, pl.ds(place % GROUP * rank_max, rank_max)],
            send_sem=send_sem.at[turn, place],
            recv_sem=recv_sem.at[turn, place],
            device_id=tile_at(-offset_of(ORDER[place])),
            device_id_type=MESH,
        )
        copy.start()
        return copy

    def spread(turn, before_first):
        copies = []
        for place in range(SLOTS):
            if turn == 0:
                load_right[place].wait()
                high, low = split(right_f32[place])
                right_hi[place] = high
                right_lo[place] = low
            coeffs[turn, place] = product(right_hi[place], right_lo[place], pair[...])
            if place == 0:
                before_first()
            else:
                copies.append(send_coeffs(turn, place - 1))
        copies.append(send_coeffs(turn, SLOTS - 1))
        return copies

    def set_pair(target, value):
        high, low = split(value)
        target[:, :cols] = high
        target[:, cols:] = low

    def diag_part(ref):
        def body(step, carry):
            at = pl.ds(pl.multiple_of(step * part, part), part)
            ref[at] = product(diag_hi[at], diag_lo[at], pair[...])
            return carry

        lax.fori_loop(0, kerns, body, 0)

    def add_group(turn, which, at, source, ref):
        lanes = pl.ds(which * depth, depth)
        ref[at] = source[at] + product(left_hi[at, lanes], left_lo[at, lanes], arrived_pair[...])

    load_rhs.wait()
    set_pair(pair, column[...])
    first_sends = spread(0, lambda: pl.semaphore_wait(barrier, SLOTS + kerns - 1))

    load_diag.wait()

    def split_diag(step, carry):
        at = pl.ds(pl.multiple_of(step * part, part), part)
        high, low = split(diag_f32[at])
        diag_hi[at] = high
        diag_lo[at] = low
        return carry

    lax.fori_loop(0, kerns, split_diag, 0)
    diag_part(total)

    load_offsets.wait()
    load_ranks.wait()
    load_left.wait()
    pad = depth - GROUP * rank_max
    for turn in range(2):
        for which in range(GROUPS):
            arrived[turn, which, pl.ds(GROUP * rank_max, pad)] = jnp.zeros((pad, cols), jnp.float32)
    for which in range(GROUPS):
        stack = []
        for place in range(which * GROUP, which * GROUP + GROUP):
            source = jnp.int32(0)
            rank = jnp.int32(0)
            for k in range(left_f32.shape[0]):
                here = offsets[0, 0, k] == offset_of(ORDER[place])
                source = jnp.where(here, k, source)
                rank = jnp.where(here, ranks[0, 0, k], rank)
            factor = left_f32[source]
            keep = lax.broadcasted_iota(jnp.int32, factor.shape, 0) < rank
            stack.append(jnp.where(keep, factor, 0.0))
        stack.append(jnp.zeros((pad, rows), jnp.float32))
        high, low = split(jnp.transpose(jnp.concatenate(stack, axis=0)))
        left_hi[:, which * depth : which * depth + depth] = high
        left_lo[:, which * depth : which * depth + depth] = low

    load_mixing.wait()
    load_index.wait()
    table_len = mixing.shape[2]
    own_index = index[pl.ds(group, 1), :]
    picker = lax.broadcasted_iota(jnp.int32, (table_len, part), 0) == own_index
    picker = jnp.transpose(picker.astype(jnp.float32))
    for a in range(kerns):
        for b in range(kerns):
            entry = jnp.broadcast_to(mixing[a, b : b + 1], (cols, table_len))
            blend[a, b] = lax.dot_general(
                picker,
                entry,
                (((1,), (1,)), ((), ())),
                precision=lax.Precision.HIGHEST,
                preferred_element_type=jnp.float32,
            )

    def collect(turn, copies, target, after):
        for which in range(GROUPS):
            for place in range(which * GROUP, which * GROUP + GROUP):
                copies[place].wait_recv()
            set_pair(arrived_pair, arrived[turn, which])
            last = which == GROUPS - 1
            for step, ahead in enumerate(turns):
                add_group(turn, which, part_rows(ahead), total, target if last else total)
                if last:
                    after(step)

    field_copies = []
    turns = tuple(sorted(range(1, kerns), key=lambda ahead: -min(ahead, kerns - ahead))) + (0,)

    def send_first(turn):
        if turn == 0:
            return
        ahead = turns[turn - 1]
        copy = pltpu.make_async_remote_copy(
            src_ref=total.at[part_rows(ahead)],
            dst_ref=gathered.at[kerns - ahead],
            send_sem=field_send.at[0, ahead],
            recv_sem=field_recv.at[0, kerns - ahead],
            device_id=kern_at(ahead),
            device_id_type=MESH,
        )
        copy.start()
        field_copies.append(copy)

    collect(0, first_sends, total, send_first)
    for copy in field_copies:
        copy.wait_recv()

    mixed_copies = []

    def send_mixed(ahead):
        copy = pltpu.make_async_remote_copy(
            src_ref=mixed_out.at[ahead],
            dst_ref=second.at[part_rows(0)],
            send_sem=field_send.at[1, ahead],
            recv_sem=field_recv.at[1, kerns - ahead],
            device_id=kern_at(ahead),
            device_id_type=MESH,
        )
        copy.start()
        mixed_copies.append(copy)

    for step, ahead in enumerate(turns):
        to = lax.rem(group + ahead, kerns)
        value = blend[to, group] * total[part_rows(0)]
        for other in range(1, kerns):
            value += blend[to, lax.rem(group + other, kerns)] * gathered[other]
        if ahead == 0:
            second[part_rows(0)] = value
        else:
            mixed_out[ahead] = value
        if step:
            send_mixed(turns[step - 1])
    for copy in field_copies:
        copy.wait_send()
    for copy in mixed_copies:
        copy.wait_recv()

    set_pair(pair, second[...])
    second_sends = spread(1, lambda: None)
    diag_part(total)
    collect(1, second_sends, out_ref, lambda step: None)
    for copy in first_sends + mixed_copies + second_sends:
        copy.wait_send()


def local(tiles, kerns, *args):
    diag, left, right, offsets, ranks, mixing, index, rhs = args
    rows, cols = rhs.shape[1:]
    count, rank_max = left.shape[2:4]
    index = index.reshape(kerns, rows // kerns)
    mixing = mixing.transpose(1, 2, 0)
    depth = -(-GROUP * rank_max // 128) * 128
    f32, bf16 = jnp.float32, jnp.bfloat16
    vmem = pltpu.VMEM
    return pl.pallas_call(
        functools.partial(kernel, tiles, kerns),
        out_shape=jax.ShapeDtypeStruct((rows, cols), f32),
        in_specs=[pl.BlockSpec(memory_space=pl.ANY)] * 8,
        out_specs=pl.BlockSpec(memory_space=pltpu.VMEM),
        scratch_shapes=[
            vmem((rows, cols), f32),
            vmem((rows, rows), f32),
            vmem((count, rank_max, rows), f32),
            vmem((SLOTS, rank_max, rows), f32),
            pltpu.SMEM(offsets.shape, jnp.int32),
            pltpu.SMEM(ranks.shape, jnp.int32),
            vmem(mixing.shape, f32),
            vmem(index.shape, jnp.int32),
            vmem((rows, rows), bf16),
            vmem((rows, rows), bf16),
            vmem((SLOTS, rank_max, rows), bf16),
            vmem((SLOTS, rank_max, rows), bf16),
            vmem((rows, GROUPS * depth), bf16),
            vmem((rows, GROUPS * depth), bf16),
            vmem((rows, 2 * cols), bf16),
            vmem((depth, 2 * cols), bf16),
            vmem((2, SLOTS, rank_max, cols), f32),
            vmem((2, GROUPS, depth, cols), f32),
            vmem((rows, cols), f32),
            vmem((kerns, kerns, rows // kerns, cols), f32),
            vmem((kerns, rows // kerns, cols), f32),
            vmem((kerns, rows // kerns, cols), f32),
            vmem((rows, cols), f32),
            pltpu.SemaphoreType.DMA((7,)),
            pltpu.SemaphoreType.DMA((SLOTS,)),
            pltpu.SemaphoreType.DMA((2, SLOTS)),
            pltpu.SemaphoreType.DMA((2, SLOTS)),
            pltpu.SemaphoreType.DMA((2, kerns)),
            pltpu.SemaphoreType.DMA((2, kerns)),
        ],
        compiler_params=pltpu.CompilerParams(collective_id=0, has_side_effects=True),
    )(diag, left, right, offsets, ranks, mixing, index, rhs)[None]


def solution(mesh):
    in_specs = (
        P("kern", "tile", None, None),
        P("kern", "tile", None, None, None),
        P("kern", "tile", None, None, None),
        P("kern", "tile", None),
        P("kern", "tile", None),
        P(),
        P("tile"),
        P("kern", "tile", None),
    )
    out_specs = P("kern", "tile", None)
    step = functools.partial(local, mesh.shape["tile"], mesh.shape["kern"])
    return jax.shard_map(step, mesh=mesh, in_specs=in_specs, out_specs=out_specs, check_vma=False)
```

```python
import functools

import jax
import jax.numpy as jnp
from jax import lax
from jax.experimental import pallas as pl
from jax.experimental.pallas import tpu as pltpu
from jax.sharding import PartitionSpec as P

MESH = pl.DeviceIdType.MESH
REACH = 6
SLOTS = 2 * REACH
ORDER = tuple(slot for far in range(REACH, 0, -1) for slot in (REACH - far, REACH + far - 1))
BLOCKS = ((0, 2), (2, 6), (6, 12))
HALVES = 2


def offset_of(slot):
    return slot - REACH if slot < REACH else slot - REACH + 1


def left_lanes(value):
    return lax.broadcasted_iota(jnp.int32, value.shape, 1) < value.shape[1] // 2


def swapped(value):
    return pltpu.roll(value, value.shape[1] // 2, 1)


def parts(value):
    high = value.astype(jnp.bfloat16)
    return high, (value - high.astype(jnp.float32)).astype(jnp.bfloat16)


def pairs(packed):
    left = left_lanes(packed)
    high = packed.astype(jnp.bfloat16).astype(jnp.float32)
    low = packed - high
    upper = jnp.where(left, high, swapped(low))
    lower = jnp.where(left, swapped(high), low)
    return upper.astype(jnp.bfloat16), lower.astype(jnp.bfloat16)


def doubled(paired):
    return paired + swapped(paired)


def packed(value):
    rows = value.shape[0] // 2
    upper = value[:rows]
    return jnp.where(left_lanes(upper), upper, value[rows:])


def dot(a, b):
    return jnp.dot(a, b, preferred_element_type=jnp.float32)


def kernel(
    tiles,
    kerns,
    diag_hbm,
    left_hbm,
    right_hbm,
    offsets_hbm,
    ranks_hbm,
    mixing_hbm,
    index_hbm,
    rhs_hbm,
    out_ref,
    column,
    diag_f32,
    left_f32,
    right_f32,
    offsets,
    ranks,
    mixing,
    index,
    diag,
    right,
    left,
    pair,
    arrived_pair,
    coeffs,
    arrived_00,
    arrived_01,
    arrived_10,
    arrived_11,
    total,
    blend,
    fields,
    gathered,
    mixed_out,
    second,
    load_sem,
    right_sem,
    send_sem,
    recv_sem,
    field_send,
    field_recv,
):
    arrived = ((arrived_00, arrived_01), (arrived_10, arrived_11))
    me = lax.axis_index("tile")
    group = lax.axis_index("kern")
    rows, cols = column.shape
    count, rank_max = left_f32.shape[:2]
    half_rank = rank_max // 2
    depth = count * half_rank
    part = rows // kerns

    def tile_at(offset):
        return (group, lax.rem(me + offset + tiles, tiles))

    def kern_of(ahead):
        return lax.rem(group + ahead, kerns)

    def lanes(half):
        return pl.ds(half * cols, cols)

    barrier = pltpu.get_barrier_semaphore()
    for slot in ORDER:
        pl.semaphore_signal(barrier, inc=1, device_id=tile_at(offset_of(slot)), device_id_type=MESH)
    for ahead in range(1, kerns):
        pl.semaphore_signal(barrier, inc=1, device_id=(kern_of(ahead), me), device_id_type=MESH)

    load_rhs = pltpu.make_async_copy(rhs_hbm.at[0], column, load_sem.at[0])
    load_rhs.start()
    load_right = []
    for place, slot in enumerate(ORDER):
        copy = pltpu.make_async_copy(right_hbm.at[0, 0, slot], right_f32.at[place], right_sem.at[place])
        copy.start()
        load_right.append(copy)
    load_diag = pltpu.make_async_copy(diag_hbm.at[0, 0], diag_f32, load_sem.at[1])
    load_left = pltpu.make_async_copy(left_hbm.at[0, 0], left_f32, load_sem.at[2])
    load_offsets = pltpu.make_async_copy(offsets_hbm, offsets, load_sem.at[3])
    load_ranks = pltpu.make_async_copy(ranks_hbm, ranks, load_sem.at[4])
    load_mixing = pltpu.make_async_copy(mixing_hbm, mixing, load_sem.at[5])
    load_index = pltpu.make_async_copy(index_hbm, index, load_sem.at[6])
    for copy in (load_diag, load_offsets, load_ranks, load_left, load_mixing, load_index):
        copy.start()

    def send_coeffs(turn, half, place):
        copy = pltpu.make_async_remote_copy(
            src_ref=coeffs.at[turn, half, place],
            dst_ref=arrived[turn][half].at[place],
            send_sem=send_sem.at[turn, half, place],
            recv_sem=recv_sem.at[turn, half, place],
            device_id=tile_at(-offset_of(ORDER[place])),
            device_id_type=MESH,
        )
        copy.start()
        return copy

    def set_pair(at, half, value):
        pair[pl.ds(at, value.shape[0]), lanes(half)] = value
        pair[pl.ds(rows + at, value.shape[0]), lanes(half)] = value

    def keep_coeffs(turn, half, first, result):
        for place in range(first, first + result.shape[0] // rank_max):
            at = (place - first) * rank_max
            coeffs[turn, half, place] = packed(doubled(result[at : at + rank_max]))

    load_rhs.wait()
    for half, value in enumerate(pairs(column[...])):
        set_pair(0, half, value)
    sends = {(0, 0): [], (0, 1): [], (1, 0): [], (1, 1): []}
    for first, end in BLOCKS:
        for place in range(first, end):
            load_right[place].wait()
            high, low = parts(right_f32[place])
            at = pl.ds(place * rank_max, rank_max)
            right[at, pl.ds(0, rows)] = high
            right[at, pl.ds(rows, rows)] = low
        result = dot(right[pl.ds(first * rank_max, (end - first) * rank_max)], pair[...])
        for half in range(HALVES):
            keep_coeffs(0, half, first, result[:, half * cols : half * cols + cols])
        if first == 0:
            pl.semaphore_wait(barrier, SLOTS + kerns - 1)
        for place in range(first, end):
            sends[0, 0].append(send_coeffs(0, 0, place))

    def diag_part():
        def body(step, carry):
            at = pl.ds(pl.multiple_of(step * 2 * part, 2 * part), 2 * part)
            result = dot(diag[at], pair[...])
            for half in range(HALVES):
                total[half, at] = result[:, half * cols : half * cols + cols]
            return carry

        lax.fori_loop(0, kerns // 2, body, 0)

    load_diag.wait()
    for step in range(kerns):
        at = pl.ds(step * part, part)
        high, low = parts(diag_f32[at])
        diag[at, pl.ds(0, rows)] = high
        diag[at, pl.ds(rows, rows)] = low
    diag_part()

    load_offsets.wait()
    load_ranks.wait()
    load_left.wait()
    places = []
    upper = []
    lower = []
    for k in range(count):
        offset = offsets[0, 0, k]
        place = 2 * (REACH - jnp.abs(offset)) + jnp.where(offset > 0, 1, 0)
        places.append(jnp.clip(place, 0, SLOTS - 1))
        factor = left_f32[k]
        keep = lax.broadcasted_iota(jnp.int32, factor.shape, 0) < ranks[0, 0, k]
        factor = jnp.where(keep, factor, 0.0)
        upper.append(factor[:half_rank])
        lower.append(factor[half_rank:])
    high, low = parts(jnp.transpose(jnp.concatenate(upper + lower, axis=0)))
    left[:, pl.ds(0, 2 * depth)] = high
    left[:, pl.ds(2 * depth, 2 * depth)] = low

    load_mixing.wait()
    load_index.wait()
    table_len = mixing.shape[2]
    own_index = index[pl.ds(group, 1), :]
    picker = lax.broadcasted_iota(jnp.int32, (table_len, part), 0) == own_index
    picker = jnp.transpose(picker.astype(jnp.float32))
    for a in range(kerns):
        weights = lax.dot_general(
            picker,
            mixing[a],
            (((1,), (1,)), ((), ())),
            precision=lax.Precision.HIGHEST,
            preferred_element_type=jnp.float32,
        )
        for b in range(kerns):
            blend[a, b] = packed(jnp.broadcast_to(weights[:, b : b + 1], (part, cols)))

    for place in range(SLOTS):
        sends[0, 1].append(send_coeffs(0, 1, place))

    def collect(turn, half):
        for place in reversed(range(SLOTS)):
            sends[turn, half][place].wait_recv()
        upper, lower = pairs(jnp.concatenate([arrived[turn][half][place] for place in places], axis=0))
        for at, value in enumerate((upper, lower, upper, lower)):
            arrived_pair[pl.ds(at * depth, depth)] = value
        total[half] += dot(left[...], arrived_pair[...])

    turns = tuple(sorted(range(1, kerns), key=lambda ahead: -min(ahead, kerns - ahead)))
    field_copies = {}

    def send_field(way, half, ahead):
        copy = pltpu.make_async_remote_copy(
            src_ref=mixed_out.at[half, ahead] if way else fields.at[half, ahead],
            dst_ref=second.at[half, group] if way else gathered.at[half, kerns - ahead],
            send_sem=field_send.at[way, half, ahead],
            recv_sem=field_recv.at[way, half, kerns - ahead],
            device_id=(kern_of(ahead), me),
            device_id_type=MESH,
        )
        copy.start()
        field_copies[way, half, ahead] = copy

    def send_first(half):
        for ahead in turns + (0,):
            at = pl.ds(pl.multiple_of(kern_of(ahead) * part, part), part)
            fields[half, ahead] = packed(doubled(total[half, at]))
        for ahead in turns:
            send_field(0, half, ahead)

    def mix(half):
        for ahead in turns:
            field_copies[0, half, ahead].wait_recv()
        for ahead in turns + (0,):
            value = blend[kern_of(ahead), group] * fields[half, 0]
            for other in range(1, kerns):
                value += blend[kern_of(ahead), kern_of(other)] * gathered[half, other]
            if ahead:
                mixed_out[half, ahead] = value
            else:
                second[half, group] = value
        for ahead in turns:
            send_field(1, half, ahead)

    def spread(half, after_second=None):
        for ahead in turns:
            field_copies[1, half, ahead].wait_recv()
        for quarter in range(kerns):
            upper, lower = pairs(second[half, quarter])
            set_pair(quarter * part, half, upper)
            set_pair(quarter * part + part // 2, half, lower)
        for step, (first, end) in enumerate(BLOCKS):
            result = dot(right[pl.ds(first * rank_max, (end - first) * rank_max)], pair[:, lanes(half)])
            keep_coeffs(1, half, first, result)
            for place in range(first, end):
                sends[1, half].append(send_coeffs(1, half, place))
            if step == 1 and after_second is not None:
                after_second()

    collect(0, 0)
    send_first(0)
    mix(0)
    collect(0, 1)
    send_first(1)
    spread(0, lambda: mix(1))
    spread(1)
    diag_part()
    for half in range(HALVES):
        collect(1, half)
    for step in range(kerns):
        at = pl.ds(step * part, part)
        value = doubled(total[0, at])
        out_ref[at] = jnp.where(left_lanes(value), value, doubled(total[1, at]))
    for copies in sends.values():
        for copy in copies:
            copy.wait_send()
    for copy in field_copies.values():
        copy.wait_send()


def local(tiles, kerns, *args):
    diag, left, right, offsets, ranks, mixing, index, rhs = args
    rows, cols = rhs.shape[1:]
    count, rank_max = left.shape[2:4]
    part = rows // kerns
    index = index.reshape(kerns, part)
    mixing = mixing.transpose(1, 2, 0)
    depth = count * rank_max // 2
    operands = (diag, left, right, offsets, ranks, mixing, index, rhs)
    operands = [pltpu.with_memory_space_constraint(value, pltpu.HBM) for value in operands]
    f32, bf16 = jnp.float32, jnp.bfloat16
    vmem = pltpu.VMEM
    return pl.pallas_call(
        functools.partial(kernel, tiles, kerns),
        out_shape=jax.ShapeDtypeStruct((rows, cols), f32),
        in_specs=[pl.BlockSpec(memory_space=pl.ANY)] * 8,
        out_specs=pl.BlockSpec(memory_space=pltpu.VMEM),
        scratch_shapes=[
            vmem((rows, cols), f32),
            vmem((rows, rows), f32),
            vmem((count, rank_max, rows), f32),
            vmem((SLOTS, rank_max, rows), f32),
            pltpu.SMEM(offsets.shape, jnp.int32),
            pltpu.SMEM(ranks.shape, jnp.int32),
            vmem(mixing.shape, f32),
            vmem(index.shape, jnp.int32),
            vmem((rows, 2 * rows), bf16),
            vmem((SLOTS * rank_max, 2 * rows), bf16),
            vmem((rows, 4 * depth), bf16),
            vmem((2 * rows, HALVES * cols), bf16),
            vmem((4 * depth, cols), bf16),
            vmem((2, HALVES, SLOTS, rank_max // 2, cols), f32),
            vmem((SLOTS, rank_max // 2, cols), f32),
            vmem((SLOTS, rank_max // 2, cols), f32),
            vmem((SLOTS, rank_max // 2, cols), f32),
            vmem((SLOTS, rank_max // 2, cols), f32),
            vmem((HALVES, rows, cols), f32),
            vmem((kerns, kerns, part // 2, cols), f32),
            vmem((HALVES, kerns, part // 2, cols), f32),
            vmem((HALVES, kerns, part // 2, cols), f32),
            vmem((HALVES, kerns, part // 2, cols), f32),
            vmem((HALVES, kerns, part // 2, cols), f32),
            pltpu.SemaphoreType.DMA((7,)),
            pltpu.SemaphoreType.DMA((SLOTS,)),
            pltpu.SemaphoreType.DMA((2, HALVES, SLOTS)),
            pltpu.SemaphoreType.DMA((2, HALVES, SLOTS)),
            pltpu.SemaphoreType.DMA((2, HALVES, kerns)),
            pltpu.SemaphoreType.DMA((2, HALVES, kerns)),
        ],
        compiler_params=pltpu.CompilerParams(collective_id=0, has_side_effects=True, vmem_limit_bytes=24 * 2**20),
    )(*operands)[None]


def solution(mesh):
    in_specs = (
        P("kern", "tile", None, None),
        P("kern", "tile", None, None, None),
        P("kern", "tile", None, None, None),
        P("kern", "tile", None),
        P("kern", "tile", None),
        P(),
        P("tile"),
        P("kern", "tile", None),
    )
    out_specs = P("kern", "tile", None)
    step = functools.partial(local, mesh.shape["tile"], mesh.shape["kern"])
    return jax.shard_map(step, mesh=mesh, in_specs=in_specs, out_specs=out_specs, check_vma=False)
```

```python
import functools

import jax
import jax.numpy as jnp
from jax import lax
from jax.experimental import pallas as pl
from jax.experimental.pallas import tpu as pltpu
from jax.sharding import PartitionSpec as P

MESH = pl.DeviceIdType.MESH
REACH = 6
SLOTS = 2 * REACH
ORDER = tuple(slot for far in range(REACH, 0, -1) for slot in (REACH - far, REACH + far - 1))
BLOCKS = ((0, 2), (2, 6), (6, 12))
HALVES = 2


def offset_of(slot):
    return slot - REACH if slot < REACH else slot - REACH + 1


def left_lanes(value):
    return lax.broadcasted_iota(jnp.int32, value.shape, 1) < value.shape[1] // 2


def swapped(value):
    return pltpu.roll(value, value.shape[1] // 2, 1)


def parts(value):
    high = value.astype(jnp.bfloat16)
    return high, (value - high.astype(jnp.float32)).astype(jnp.bfloat16)


def pairs(packed):
    left = left_lanes(packed)
    high = packed.astype(jnp.bfloat16).astype(jnp.float32)
    low = packed - high
    upper = jnp.where(left, high, swapped(low))
    lower = jnp.where(left, swapped(high), low)
    return upper.astype(jnp.bfloat16), lower.astype(jnp.bfloat16)


def doubled(paired):
    return paired + swapped(paired)


def packed(value):
    rows = value.shape[0] // 2
    upper = value[:rows]
    return jnp.where(left_lanes(upper), upper, value[rows:])


def dot(a, b):
    return jnp.dot(a, b, preferred_element_type=jnp.float32)


def kernel(
    tiles,
    kerns,
    diag_hbm,
    left_hbm,
    right_hbm,
    offsets_hbm,
    ranks_hbm,
    mixing_hbm,
    index_hbm,
    rhs_hbm,
    out_ref,
    column,
    diag_f32,
    left_f32,
    right_f32,
    offsets,
    ranks,
    mixing,
    index,
    diag,
    right,
    left,
    pair,
    arrived_pair,
    coeffs,
    arrived_00,
    arrived_01,
    arrived_10,
    arrived_11,
    total,
    blend,
    fields,
    gathered,
    mixed_out,
    second,
    load_sem,
    right_sem,
    send_sem,
    recv_sem,
    field_send,
    field_recv,
):
    arrived = ((arrived_00, arrived_01), (arrived_10, arrived_11))
    me = lax.axis_index("tile")
    group = lax.axis_index("kern")
    rows, cols = column.shape
    count, rank_max = left_f32.shape[:2]
    half_rank = rank_max // 2
    depth = count * half_rank
    part = rows // kerns

    def tile_at(offset):
        return (group, lax.rem(me + offset + tiles, tiles))

    def kern_of(ahead):
        return lax.rem(group + ahead, kerns)

    def lanes(half):
        return pl.ds(half * cols, cols)

    load_rhs = pltpu.make_async_copy(rhs_hbm.at[0], column, load_sem.at[0])
    load_rhs.start()

    def right_block(block):
        first, end = BLOCKS[block]
        at = right_f32.at[pl.ds(first, end - first)]
        return pltpu.make_async_copy(at, at, right_sem.at[block])

    def load_right(block):
        for place in range(*BLOCKS[block]):
            source = right_hbm.at[0, 0, ORDER[place]]
            pltpu.make_async_copy(source, right_f32.at[place], right_sem.at[block]).start()

    load_right(0)

    barrier = pltpu.get_barrier_semaphore()
    for slot in ORDER:
        pl.semaphore_signal(barrier, inc=1, device_id=tile_at(offset_of(slot)), device_id_type=MESH)
    for ahead in range(1, kerns):
        pl.semaphore_signal(barrier, inc=1, device_id=(kern_of(ahead), me), device_id_type=MESH)

    for block in range(1, len(BLOCKS)):
        load_right(block)
    load_diag = pltpu.make_async_copy(diag_hbm.at[0, 0], diag_f32, load_sem.at[1])
    load_left = pltpu.make_async_copy(left_hbm.at[0, 0], left_f32, load_sem.at[2])
    load_offsets = pltpu.make_async_copy(offsets_hbm, offsets, load_sem.at[3])
    load_ranks = pltpu.make_async_copy(ranks_hbm, ranks, load_sem.at[4])
    load_mixing = pltpu.make_async_copy(mixing_hbm, mixing, load_sem.at[5])
    load_index = pltpu.make_async_copy(index_hbm, index, load_sem.at[6])
    for copy in (load_diag, load_offsets, load_ranks, load_left, load_mixing, load_index):
        copy.start()

    def send_coeffs(turn, half, place):
        copy = pltpu.make_async_remote_copy(
            src_ref=coeffs.at[turn, half, place],
            dst_ref=arrived[turn][half].at[place],
            send_sem=send_sem,
            recv_sem=recv_sem.at[turn, half],
            device_id=tile_at(-offset_of(ORDER[place])),
            device_id_type=MESH,
        )
        copy.start()

    def set_pair(at, half, value):
        pair[pl.ds(at, value.shape[0]), lanes(half)] = value
        pair[pl.ds(rows + at, value.shape[0]), lanes(half)] = value

    def keep_coeffs(turn, half, first, result):
        for place in range(first, first + result.shape[0] // rank_max):
            at = (place - first) * rank_max
            coeffs[turn, half, place] = packed(doubled(result[at : at + rank_max]))

    load_rhs.wait()
    for half, value in enumerate(pairs(column[...])):
        set_pair(0, half, value)
    for block, (first, end) in enumerate(BLOCKS):
        right_block(block).wait()
        for place in range(first, end):
            high, low = parts(right_f32[place])
            at = pl.ds(place * rank_max, rank_max)
            right[at, pl.ds(0, rows)] = high
            right[at, pl.ds(rows, rows)] = low
        result = dot(right[pl.ds(first * rank_max, (end - first) * rank_max)], pair[...])
        for half in range(HALVES):
            keep_coeffs(0, half, first, result[:, half * cols : half * cols + cols])
        if first == 0:
            pl.semaphore_wait(barrier, SLOTS + kerns - 1)
        for place in range(first, end):
            send_coeffs(0, 0, place)

    def diag_part():
        def body(step, carry):
            at = pl.ds(pl.multiple_of(step * 2 * part, 2 * part), 2 * part)
            result = dot(diag[at], pair[...])
            for half in range(HALVES):
                total[half, at] = result[:, half * cols : half * cols + cols]
            return carry

        lax.fori_loop(0, kerns // 2, body, 0)

    load_diag.wait()
    for step in range(kerns):
        at = pl.ds(step * part, part)
        high, low = parts(diag_f32[at])
        diag[at, pl.ds(0, rows)] = high
        diag[at, pl.ds(rows, rows)] = low
    diag_part()

    load_offsets.wait()
    load_ranks.wait()
    load_left.wait()
    places = []
    upper = []
    lower = []
    for k in range(count):
        offset = offsets[0, 0, k]
        place = 2 * (REACH - jnp.abs(offset)) + jnp.where(offset > 0, 1, 0)
        places.append(jnp.clip(place, 0, SLOTS - 1))
        factor = left_f32[k]
        keep = lax.broadcasted_iota(jnp.int32, factor.shape, 0) < ranks[0, 0, k]
        factor = jnp.where(keep, factor, 0.0)
        upper.append(factor[:half_rank])
        lower.append(factor[half_rank:])
    high, low = parts(jnp.transpose(jnp.concatenate(upper + lower, axis=0)))
    left[:, pl.ds(0, 2 * depth)] = high
    left[:, pl.ds(2 * depth, 2 * depth)] = low

    load_mixing.wait()
    load_index.wait()
    table_len = mixing.shape[2]
    own_index = index[pl.ds(group, 1), :]
    picker = lax.broadcasted_iota(jnp.int32, (table_len, part), 0) == own_index
    picker = jnp.transpose(picker.astype(jnp.float32))
    for a in range(kerns):
        weights = lax.dot_general(
            picker,
            mixing[a],
            (((1,), (1,)), ((), ())),
            precision=lax.Precision.HIGHEST,
            preferred_element_type=jnp.float32,
        )
        for b in range(kerns):
            blend[a, b] = packed(jnp.broadcast_to(weights[:, b : b + 1], (part, cols)))

    for place in range(SLOTS):
        send_coeffs(0, 1, place)

    def collect(turn, half):
        buffer = arrived[turn][half]
        pltpu.make_async_copy(buffer, buffer, recv_sem.at[turn, half]).wait()
        upper, lower = pairs(jnp.concatenate([buffer[place] for place in places], axis=0))
        for at, value in enumerate((upper, lower, upper, lower)):
            arrived_pair[pl.ds(at * depth, depth)] = value
        total[half] += dot(left[...], arrived_pair[...])

    turns = tuple(sorted(range(1, kerns), key=lambda ahead: -min(ahead, kerns - ahead)))

    def wait_fields(way, half):
        size = gathered.at[half, pl.ds(1, kerns - 1)]
        pltpu.make_async_copy(size, size, field_recv.at[way, half]).wait()

    def send_field(way, half, ahead):
        copy = pltpu.make_async_remote_copy(
            src_ref=mixed_out.at[half, ahead] if way else fields.at[half, ahead],
            dst_ref=second.at[half, group] if way else gathered.at[half, kerns - ahead],
            send_sem=field_send.at[way],
            recv_sem=field_recv.at[way, half],
            device_id=(kern_of(ahead), me),
            device_id_type=MESH,
        )
        copy.start()

    def send_first(half):
        for ahead in turns + (0,):
            at = pl.ds(pl.multiple_of(kern_of(ahead) * part, part), part)
            fields[half, ahead] = packed(doubled(total[half, at]))
        for ahead in turns:
            send_field(0, half, ahead)

    def mix(half):
        wait_fields(0, half)
        for ahead in turns + (0,):
            value = blend[kern_of(ahead), group] * fields[half, 0]
            for other in range(1, kerns):
                value += blend[kern_of(ahead), kern_of(other)] * gathered[half, other]
            if ahead:
                mixed_out[half, ahead] = value
            else:
                second[half, group] = value
        for ahead in turns:
            send_field(1, half, ahead)

    def spread(half, after_second=None):
        wait_fields(1, half)
        for quarter in range(kerns):
            upper, lower = pairs(second[half, quarter])
            set_pair(quarter * part, half, upper)
            set_pair(quarter * part + part // 2, half, lower)
        for step, (first, end) in enumerate(BLOCKS):
            result = dot(right[pl.ds(first * rank_max, (end - first) * rank_max)], pair[:, lanes(half)])
            keep_coeffs(1, half, first, result)
            for place in range(first, end):
                send_coeffs(1, half, place)
            if step == 1 and after_second is not None:
                after_second()

    collect(0, 0)
    send_first(0)
    mix(0)
    collect(0, 1)
    send_first(1)
    spread(0, lambda: mix(1))
    spread(1)
    diag_part()
    for half in range(HALVES):
        collect(1, half)
    for step in range(kerns):
        at = pl.ds(step * part, part)
        value = doubled(total[0, at])
        out_ref[at] = jnp.where(left_lanes(value), value, doubled(total[1, at]))
    pltpu.make_async_copy(coeffs, coeffs, send_sem).wait()
    for way, ref in enumerate((fields, mixed_out)):
        size = ref.at[:, pl.ds(1, kerns - 1)]
        pltpu.make_async_copy(size, size, field_send.at[way]).wait()


def local(tiles, kerns, *args):
    diag, left, right, offsets, ranks, mixing, index, rhs = args
    rows, cols = rhs.shape[1:]
    count, rank_max = left.shape[2:4]
    part = rows // kerns
    index = index.reshape(kerns, part)
    mixing = mixing.transpose(1, 2, 0)
    depth = count * rank_max // 2
    operands = (diag, left, right, offsets, ranks, mixing, index, rhs)
    operands = [pltpu.with_memory_space_constraint(value, pltpu.HBM) for value in operands]
    f32, bf16 = jnp.float32, jnp.bfloat16
    vmem = pltpu.VMEM
    return pl.pallas_call(
        functools.partial(kernel, tiles, kerns),
        out_shape=jax.ShapeDtypeStruct((rows, cols), f32),
        in_specs=[pl.BlockSpec(memory_space=pl.ANY)] * 8,
        out_specs=pl.BlockSpec(memory_space=pltpu.VMEM),
        scratch_shapes=[
            vmem((rows, cols), f32),
            vmem((rows, rows), f32),
            vmem((count, rank_max, rows), f32),
            vmem((SLOTS, rank_max, rows), f32),
            pltpu.SMEM(offsets.shape, jnp.int32),
            pltpu.SMEM(ranks.shape, jnp.int32),
            vmem(mixing.shape, f32),
            vmem(index.shape, jnp.int32),
            vmem((rows, 2 * rows), bf16),
            vmem((SLOTS * rank_max, 2 * rows), bf16),
            vmem((rows, 4 * depth), bf16),
            vmem((2 * rows, HALVES * cols), bf16),
            vmem((4 * depth, cols), bf16),
            vmem((2, HALVES, SLOTS, rank_max // 2, cols), f32),
            vmem((SLOTS, rank_max // 2, cols), f32),
            vmem((SLOTS, rank_max // 2, cols), f32),
            vmem((SLOTS, rank_max // 2, cols), f32),
            vmem((SLOTS, rank_max // 2, cols), f32),
            vmem((HALVES, rows, cols), f32),
            vmem((kerns, kerns, part // 2, cols), f32),
            vmem((HALVES, kerns, part // 2, cols), f32),
            vmem((HALVES, kerns, part // 2, cols), f32),
            vmem((HALVES, kerns, part // 2, cols), f32),
            vmem((HALVES, kerns, part // 2, cols), f32),
            pltpu.SemaphoreType.DMA((7,)),
            pltpu.SemaphoreType.DMA((len(BLOCKS),)),
            pltpu.SemaphoreType.DMA,
            pltpu.SemaphoreType.DMA((2, HALVES)),
            pltpu.SemaphoreType.DMA((2,)),
            pltpu.SemaphoreType.DMA((2, HALVES)),
        ],
        compiler_params=pltpu.CompilerParams(collective_id=0, has_side_effects=True, vmem_limit_bytes=24 * 2**20),
    )(*operands)[None]


def solution(mesh):
    in_specs = (
        P("kern", "tile", None, None),
        P("kern", "tile", None, None, None),
        P("kern", "tile", None, None, None),
        P("kern", "tile", None),
        P("kern", "tile", None),
        P(),
        P("tile"),
        P("kern", "tile", None),
    )
    out_specs = P("kern", "tile", None)
    step = functools.partial(local, mesh.shape["tile"], mesh.shape["kern"])
    return jax.shard_map(step, mesh=mesh, in_specs=in_specs, out_specs=out_specs, check_vma=False)
```

```python
import functools

import jax
import jax.numpy as jnp
from jax import lax
from jax.experimental import pallas as pl
from jax.experimental.pallas import tpu as pltpu
from jax.sharding import PartitionSpec as P

MESH = pl.DeviceIdType.MESH
REACH = 6
SLOTS = 2 * REACH
ORDER = tuple(slot for far in range(REACH, 0, -1) for slot in (REACH - far, REACH + far - 1))
BLOCKS = ((0, 2), (2, 6), (6, 12))
HALVES = 2
PIECES = 2


def offset_of(slot):
    return slot - REACH if slot < REACH else slot - REACH + 1


def left_lanes(value):
    return lax.broadcasted_iota(jnp.int32, value.shape, 1) < value.shape[1] // 2


def swapped(value):
    return pltpu.roll(value, value.shape[1] // 2, 1)


def parts(value):
    high = value.astype(jnp.bfloat16)
    return high, (value - high.astype(jnp.float32)).astype(jnp.bfloat16)


def pairs(packed):
    left = left_lanes(packed)
    high = packed.astype(jnp.bfloat16).astype(jnp.float32)
    low = packed - high
    upper = jnp.where(left, high, swapped(low))
    lower = jnp.where(left, swapped(high), low)
    return upper.astype(jnp.bfloat16), lower.astype(jnp.bfloat16)


def doubled(paired):
    return paired + swapped(paired)


def packed(value):
    rows = value.shape[0] // 2
    upper = value[:rows]
    return jnp.where(left_lanes(upper), upper, value[rows:])


def dot(a, b):
    return jnp.dot(a, b, preferred_element_type=jnp.float32)


def kernel(
    tiles,
    kerns,
    diag_hbm,
    left_hbm,
    right_hbm,
    offsets_hbm,
    ranks_hbm,
    mixing_hbm,
    index_hbm,
    rhs_hbm,
    out_ref,
    column,
    diag_f32,
    left_f32,
    right_f32,
    offsets,
    ranks,
    mixing,
    index,
    diag,
    right,
    left,
    pair,
    arrived_pair,
    coeffs,
    arrived_00,
    arrived_01,
    arrived_10,
    arrived_11,
    total,
    blend,
    fields,
    gathered,
    mixed_out,
    second,
    load_sem,
    right_sem,
    send_sem,
    recv_sem,
    field_send,
    field_recv,
):
    arrived = ((arrived_00, arrived_01), (arrived_10, arrived_11))
    me = lax.axis_index("tile")
    group = lax.axis_index("kern")
    rows, cols = column.shape
    count, rank_max = left_f32.shape[:2]
    half_rank = rank_max // 2
    depth = count * half_rank
    part = rows // kerns

    def tile_at(offset):
        return (group, lax.rem(me + offset + tiles, tiles))

    def kern_of(ahead):
        return lax.rem(group + ahead, kerns)

    def lanes(half):
        return pl.ds(half * cols, cols)

    load_rhs = pltpu.make_async_copy(rhs_hbm.at[0], column, load_sem.at[0])
    load_rhs.start()

    def right_block(block):
        first, end = BLOCKS[block]
        at = right_f32.at[pl.ds(first, end - first)]
        return pltpu.make_async_copy(at, at, right_sem.at[block])

    def load_right(block):
        for place in range(*BLOCKS[block]):
            source = right_hbm.at[0, 0, ORDER[place]]
            pltpu.make_async_copy(source, right_f32.at[place], right_sem.at[block]).start()

    load_right(0)

    barrier = pltpu.get_barrier_semaphore()
    for slot in ORDER:
        pl.semaphore_signal(barrier, inc=1, device_id=tile_at(offset_of(slot)), device_id_type=MESH)
    for ahead in range(1, kerns):
        pl.semaphore_signal(barrier, inc=1, device_id=(kern_of(ahead), me), device_id_type=MESH)

    for block in range(1, len(BLOCKS)):
        load_right(block)
    load_diag = pltpu.make_async_copy(diag_hbm.at[0, 0], diag_f32, load_sem.at[1])
    load_left = pltpu.make_async_copy(left_hbm.at[0, 0], left_f32, load_sem.at[2])
    load_offsets = pltpu.make_async_copy(offsets_hbm, offsets, load_sem.at[3])
    load_ranks = pltpu.make_async_copy(ranks_hbm, ranks, load_sem.at[4])
    load_mixing = pltpu.make_async_copy(mixing_hbm, mixing, load_sem.at[5])
    load_index = pltpu.make_async_copy(index_hbm, index, load_sem.at[6])
    for copy in (load_diag, load_offsets, load_ranks, load_left, load_mixing, load_index):
        copy.start()

    def send_coeffs(turn, half, place):
        copy = pltpu.make_async_remote_copy(
            src_ref=coeffs.at[turn, half, place],
            dst_ref=arrived[turn][half].at[place],
            send_sem=send_sem,
            recv_sem=recv_sem.at[turn, half],
            device_id=tile_at(-offset_of(ORDER[place])),
            device_id_type=MESH,
        )
        copy.start()

    def set_pair(at, half, value):
        pair[pl.ds(at, value.shape[0]), lanes(half)] = value
        pair[pl.ds(rows + at, value.shape[0]), lanes(half)] = value

    def keep_coeffs(turn, half, first, result):
        for place in range(first, first + result.shape[0] // rank_max):
            at = (place - first) * rank_max
            coeffs[turn, half, place] = packed(doubled(result[at : at + rank_max]))

    load_rhs.wait()
    for half, value in enumerate(pairs(column[...])):
        set_pair(0, half, value)
    for block, (first, end) in enumerate(BLOCKS):
        right_block(block).wait()
        for place in range(first, end):
            high, low = parts(right_f32[place])
            at = pl.ds(place * rank_max, rank_max)
            right[at, pl.ds(0, rows)] = high
            right[at, pl.ds(rows, rows)] = low
        result = dot(right[pl.ds(first * rank_max, (end - first) * rank_max)], pair[...])
        for half in range(HALVES):
            keep_coeffs(0, half, first, result[:, half * cols : half * cols + cols])
        if block == 1:
            pl.semaphore_wait(barrier, SLOTS + kerns - 1)
            first = 0
        if block:
            for place in range(first, end):
                send_coeffs(0, 0, place)

    def diag_part():
        def body(step, carry):
            at = pl.ds(pl.multiple_of(step * 2 * part, 2 * part), 2 * part)
            result = dot(diag[at], pair[...])
            for half in range(HALVES):
                total[half, at] = result[:, half * cols : half * cols + cols]
            return carry

        lax.fori_loop(0, kerns // 2, body, 0)

    load_diag.wait()
    for step in range(kerns):
        at = pl.ds(step * part, part)
        high, low = parts(diag_f32[at])
        diag[at, pl.ds(0, rows)] = high
        diag[at, pl.ds(rows, rows)] = low
    diag_part()

    load_offsets.wait()
    load_ranks.wait()
    load_left.wait()
    places = []
    upper = []
    lower = []
    for k in range(count):
        offset = offsets[0, 0, k]
        place = 2 * (REACH - jnp.abs(offset)) + jnp.where(offset > 0, 1, 0)
        places.append(jnp.clip(place, 0, SLOTS - 1))
        factor = left_f32[k]
        keep = lax.broadcasted_iota(jnp.int32, factor.shape, 0) < ranks[0, 0, k]
        factor = jnp.where(keep, factor, 0.0)
        upper.append(factor[:half_rank])
        lower.append(factor[half_rank:])
    high, low = parts(jnp.transpose(jnp.concatenate(upper + lower, axis=0)))
    left[:, pl.ds(0, 2 * depth)] = high
    left[:, pl.ds(2 * depth, 2 * depth)] = low

    load_mixing.wait()
    load_index.wait()
    table_len = mixing.shape[2]
    own_index = index[pl.ds(group, 1), :]
    picker = lax.broadcasted_iota(jnp.int32, (table_len, part), 0) == own_index
    picker = jnp.transpose(picker.astype(jnp.float32))
    for a in range(kerns):
        weights = lax.dot_general(
            picker,
            mixing[a],
            (((1,), (1,)), ((), ())),
            precision=lax.Precision.HIGHEST,
            preferred_element_type=jnp.float32,
        )
        for b in range(kerns):
            blend[a, b] = packed(jnp.broadcast_to(weights[:, b : b + 1], (part, cols)))

    for place in range(SLOTS):
        send_coeffs(0, 1, place)

    def collect(turn, half):
        buffer = arrived[turn][half]
        pltpu.make_async_copy(buffer, buffer, recv_sem.at[turn, half]).wait()
        upper, lower = pairs(jnp.concatenate([buffer[place] for place in places], axis=0))
        for at, value in enumerate((upper, lower, upper, lower)):
            arrived_pair[pl.ds(at * depth, depth)] = value
        total[half] += dot(left[...], arrived_pair[...])

    turns = tuple(sorted(range(1, kerns), key=lambda ahead: -min(ahead, kerns - ahead)))

    rest = part // 2 // PIECES

    def wait_fields(way, half, piece):
        size = gathered.at[half, pl.ds(1, kerns - 1), pl.ds(piece * rest, rest)]
        pltpu.make_async_copy(size, size, field_recv.at[way, half, piece]).wait()

    def send_field(way, half, ahead, piece):
        at = pl.ds(piece * rest, rest)
        copy = pltpu.make_async_remote_copy(
            src_ref=mixed_out.at[half, ahead, at] if way else fields.at[half, ahead, at],
            dst_ref=second.at[half, group, at] if way else gathered.at[half, kerns - ahead, at],
            send_sem=field_send.at[way],
            recv_sem=field_recv.at[way, half, piece],
            device_id=(kern_of(ahead), me),
            device_id_type=MESH,
        )
        copy.start()

    def send_first(half):
        for ahead in turns + (0,):
            at = pl.ds(pl.multiple_of(kern_of(ahead) * part, part), part)
            fields[half, ahead] = packed(doubled(total[half, at]))
        for piece in range(PIECES):
            for ahead in turns:
                send_field(0, half, ahead, piece)

    def mix(half):
        for piece in range(PIECES):
            at = pl.ds(piece * rest, rest)
            wait_fields(0, half, piece)
            for ahead in turns + (0,):
                value = blend[kern_of(ahead), group, at] * fields[half, 0, at]
                for other in range(1, kerns):
                    value += blend[kern_of(ahead), kern_of(other), at] * gathered[half, other, at]
                if ahead:
                    mixed_out[half, ahead, at] = value
                else:
                    second[half, group, at] = value
            for ahead in turns:
                send_field(1, half, ahead, piece)

    def spread(half, after_second=None):
        for piece in range(PIECES):
            wait_fields(1, half, piece)
        for quarter in range(kerns):
            upper, lower = pairs(second[half, quarter])
            set_pair(quarter * part, half, upper)
            set_pair(quarter * part + part // 2, half, lower)
        for step, (first, end) in enumerate(BLOCKS):
            result = dot(right[pl.ds(first * rank_max, (end - first) * rank_max)], pair[:, lanes(half)])
            keep_coeffs(1, half, first, result)
            for place in range(first, end):
                send_coeffs(1, half, place)
            if step == 1 and after_second is not None:
                after_second()

    collect(0, 0)
    send_first(0)
    mix(0)
    collect(0, 1)
    send_first(1)
    spread(0, lambda: mix(1))
    spread(1)
    diag_part()
    collect(1, 0)
    for step in range(kerns):
        at = pl.ds(step * part, part)
        total[0, at] = doubled(total[0, at])
    collect(1, 1)
    for step in range(kerns):
        at = pl.ds(step * part, part)
        value = total[0, at]
        out_ref[at] = jnp.where(left_lanes(value), value, doubled(total[1, at]))
    pltpu.make_async_copy(coeffs, coeffs, send_sem).wait()
    for way, ref in enumerate((fields, mixed_out)):
        size = ref.at[:, pl.ds(1, kerns - 1)]
        pltpu.make_async_copy(size, size, field_send.at[way]).wait()


def local(tiles, kerns, *args):
    diag, left, right, offsets, ranks, mixing, index, rhs = args
    rows, cols = rhs.shape[1:]
    count, rank_max = left.shape[2:4]
    part = rows // kerns
    index = index.reshape(kerns, part)
    mixing = mixing.transpose(1, 2, 0)
    depth = count * rank_max // 2
    operands = (diag, left, right, offsets, ranks, mixing, index, rhs)
    operands = [pltpu.with_memory_space_constraint(value, pltpu.HBM) for value in operands]
    f32, bf16 = jnp.float32, jnp.bfloat16
    vmem = pltpu.VMEM
    return pl.pallas_call(
        functools.partial(kernel, tiles, kerns),
        out_shape=jax.ShapeDtypeStruct((rows, cols), f32),
        in_specs=[pl.BlockSpec(memory_space=pl.ANY)] * 8,
        out_specs=pl.BlockSpec(memory_space=pltpu.VMEM),
        scratch_shapes=[
            vmem((rows, cols), f32),
            vmem((rows, rows), f32),
            vmem((count, rank_max, rows), f32),
            vmem((SLOTS, rank_max, rows), f32),
            pltpu.SMEM(offsets.shape, jnp.int32),
            pltpu.SMEM(ranks.shape, jnp.int32),
            vmem(mixing.shape, f32),
            vmem(index.shape, jnp.int32),
            vmem((rows, 2 * rows), bf16),
            vmem((SLOTS * rank_max, 2 * rows), bf16),
            vmem((rows, 4 * depth), bf16),
            vmem((2 * rows, HALVES * cols), bf16),
            vmem((4 * depth, cols), bf16),
            vmem((2, HALVES, SLOTS, rank_max // 2, cols), f32),
            vmem((SLOTS, rank_max // 2, cols), f32),
            vmem((SLOTS, rank_max // 2, cols), f32),
            vmem((SLOTS, rank_max // 2, cols), f32),
            vmem((SLOTS, rank_max // 2, cols), f32),
            vmem((HALVES, rows, cols), f32),
            vmem((kerns, kerns, part // 2, cols), f32),
            vmem((HALVES, kerns, part // 2, cols), f32),
            vmem((HALVES, kerns, part // 2, cols), f32),
            vmem((HALVES, kerns, part // 2, cols), f32),
            vmem((HALVES, kerns, part // 2, cols), f32),
            pltpu.SemaphoreType.DMA((7,)),
            pltpu.SemaphoreType.DMA((len(BLOCKS),)),
            pltpu.SemaphoreType.DMA,
            pltpu.SemaphoreType.DMA((2, HALVES)),
            pltpu.SemaphoreType.DMA((2,)),
            pltpu.SemaphoreType.DMA((2, HALVES, PIECES)),
        ],
        compiler_params=pltpu.CompilerParams(collective_id=0, has_side_effects=True, vmem_limit_bytes=24 * 2**20),
    )(*operands)[None]


def solution(mesh):
    in_specs = (
        P("kern", "tile", None, None),
        P("kern", "tile", None, None, None),
        P("kern", "tile", None, None, None),
        P("kern", "tile", None),
        P("kern", "tile", None),
        P(),
        P("tile"),
        P("kern", "tile", None),
    )
    out_specs = P("kern", "tile", None)
    step = functools.partial(local, mesh.shape["tile"], mesh.shape["kern"])
    return jax.shard_map(step, mesh=mesh, in_specs=in_specs, out_specs=out_specs, check_vma=False)
```

```python
import functools

import jax
import jax.numpy as jnp
from jax import lax
from jax.experimental import pallas as pl
from jax.experimental.pallas import tpu as pltpu
from jax.sharding import PartitionSpec as P

MESH = pl.DeviceIdType.MESH
REACH = 6
SLOTS = 2 * REACH
ORDER = tuple(slot for far in range(REACH, 0, -1) for slot in (REACH - far, REACH + far - 1))
BLOCKS = ((0, 2), (2, 6), (6, 12))
HALVES = 2
PIECES = 2


def offset_of(slot):
    return slot - REACH if slot < REACH else slot - REACH + 1


def left_lanes(value):
    return lax.broadcasted_iota(jnp.int32, value.shape, 1) < value.shape[1] // 2


def swapped(value):
    return pltpu.roll(value, value.shape[1] // 2, 1)


def parts(value):
    high = value.astype(jnp.bfloat16)
    return high, (value - high.astype(jnp.float32)).astype(jnp.bfloat16)


def pairs(packed):
    left = left_lanes(packed)
    high = packed.astype(jnp.bfloat16).astype(jnp.float32)
    low = packed - high
    upper = jnp.where(left, high, swapped(low))
    lower = jnp.where(left, swapped(high), low)
    return upper.astype(jnp.bfloat16), lower.astype(jnp.bfloat16)


def doubled(paired):
    return paired + swapped(paired)


def packed(value):
    rows = value.shape[0] // 2
    upper = value[:rows]
    return jnp.where(left_lanes(upper), upper, value[rows:])


def dot(a, b):
    return jnp.dot(a, b, preferred_element_type=jnp.float32)


def kernel(
    tiles,
    kerns,
    diag_hbm,
    left_hbm,
    right_hbm,
    offsets_hbm,
    ranks_hbm,
    mixing_hbm,
    index_hbm,
    rhs_hbm,
    out_ref,
    column,
    diag_f32,
    left_f32,
    right_f32,
    offsets,
    ranks,
    mixing,
    index,
    diag,
    right,
    left,
    pair,
    arrived_pair,
    coeffs,
    arrived_00,
    arrived_01,
    arrived_10,
    arrived_11,
    total,
    blend,
    fields,
    gathered,
    mixed_out,
    second,
    load_sem,
    right_sem,
    send_sem,
    recv_sem,
    field_send,
    field_recv,
):
    arrived = ((arrived_00, arrived_01), (arrived_10, arrived_11))
    me = lax.axis_index("tile")
    group = lax.axis_index("kern")
    rows, cols = column.shape
    count, rank_max = left_f32.shape[:2]
    half_rank = rank_max // 2
    depth = count * half_rank
    part = rows // kerns

    def tile_at(offset):
        return (group, lax.rem(me + offset + tiles, tiles))

    def kern_of(ahead):
        return lax.rem(group + ahead, kerns)

    def lanes(half):
        return pl.ds(half * cols, cols)

    load_rhs = pltpu.make_async_copy(rhs_hbm.at[0], column, load_sem.at[0])
    load_rhs.start()

    def right_block(block):
        first, end = BLOCKS[block]
        at = right_f32.at[pl.ds(first, end - first)]
        return pltpu.make_async_copy(at, at, right_sem.at[block])

    def load_right(block):
        for place in range(*BLOCKS[block]):
            source = right_hbm.at[0, 0, ORDER[place]]
            pltpu.make_async_copy(source, right_f32.at[place], right_sem.at[block]).start()

    load_right(0)

    barrier = pltpu.get_barrier_semaphore()
    for slot in ORDER:
        pl.semaphore_signal(barrier, inc=1, device_id=tile_at(offset_of(slot)), device_id_type=MESH)
    for ahead in range(1, kerns):
        pl.semaphore_signal(barrier, inc=1, device_id=(kern_of(ahead), me), device_id_type=MESH)

    for block in range(1, len(BLOCKS)):
        load_right(block)
    load_diag = pltpu.make_async_copy(diag_hbm.at[0, 0], diag_f32, load_sem.at[1])
    load_left = pltpu.make_async_copy(left_hbm.at[0, 0], left_f32, load_sem.at[2])
    load_offsets = pltpu.make_async_copy(offsets_hbm, offsets, load_sem.at[3])
    load_ranks = pltpu.make_async_copy(ranks_hbm, ranks, load_sem.at[4])
    load_mixing = pltpu.make_async_copy(mixing_hbm, mixing, load_sem.at[5])
    load_index = pltpu.make_async_copy(index_hbm, index, load_sem.at[6])
    for copy in (load_diag, load_offsets, load_ranks, load_left, load_mixing, load_index):
        copy.start()

    def send_coeffs(turn, half, place):
        copy = pltpu.make_async_remote_copy(
            src_ref=coeffs.at[turn, half, place],
            dst_ref=arrived[turn][half].at[place],
            send_sem=send_sem,
            recv_sem=recv_sem.at[turn, half],
            device_id=tile_at(-offset_of(ORDER[place])),
            device_id_type=MESH,
        )
        copy.start()

    def set_pair(at, half, value):
        pair[pl.ds(at, value.shape[0]), lanes(half)] = value
        pair[pl.ds(rows + at, value.shape[0]), lanes(half)] = value

    def keep_coeffs(turn, half, first, result):
        for place in range(first, first + result.shape[0] // rank_max):
            at = (place - first) * rank_max
            coeffs[turn, half, place] = packed(doubled(result[at : at + rank_max]))

    load_rhs.wait()
    for half, value in enumerate(pairs(column[...])):
        set_pair(0, half, value)
    for block, (first, end) in enumerate(BLOCKS):
        right_block(block).wait()
        for place in range(first, end):
            high, low = parts(right_f32[place])
            at = pl.ds(place * rank_max, rank_max)
            right[at, pl.ds(0, rows)] = high
            right[at, pl.ds(rows, rows)] = low
        result = dot(right[pl.ds(first * rank_max, (end - first) * rank_max)], pair[...])
        for half in range(HALVES):
            keep_coeffs(0, half, first, result[:, half * cols : half * cols + cols])
        if block == 1:
            pl.semaphore_wait(barrier, SLOTS + kerns - 1)
            first = 0
        if block:
            for place in range(first, end):
                send_coeffs(0, 0, place)

    def diag_part():
        def body(step, carry):
            at = pl.ds(pl.multiple_of(step * 2 * part, 2 * part), 2 * part)
            result = dot(diag[at], pair[...])
            for half in range(HALVES):
                total[half, at] = result[:, half * cols : half * cols + cols]
            return carry

        lax.fori_loop(0, kerns // 2, body, 0)

    load_diag.wait()
    for step in range(kerns):
        at = pl.ds(step * part, part)
        high, low = parts(diag_f32[at])
        diag[at, pl.ds(0, rows)] = high
        diag[at, pl.ds(rows, rows)] = low
    diag_part()

    load_offsets.wait()
    load_ranks.wait()
    load_left.wait()
    places = []
    upper = []
    lower = []
    for k in range(count):
        offset = offsets[0, 0, k]
        place = 2 * (REACH - jnp.abs(offset)) + jnp.where(offset > 0, 1, 0)
        places.append(jnp.clip(place, 0, SLOTS - 1))
        factor = left_f32[k]
        keep = lax.broadcasted_iota(jnp.int32, factor.shape, 0) < ranks[0, 0, k]
        factor = jnp.where(keep, factor, 0.0)
        upper.append(factor[:half_rank])
        lower.append(factor[half_rank:])
    high, low = parts(jnp.transpose(jnp.concatenate(upper + lower, axis=0)))
    left[:, pl.ds(0, 2 * depth)] = high
    left[:, pl.ds(2 * depth, 2 * depth)] = low

    load_mixing.wait()
    load_index.wait()
    table_len = mixing.shape[2]
    own_index = index[pl.ds(group, 1), :]
    picker = lax.broadcasted_iota(jnp.int32, (table_len, part), 0) == own_index
    picker = jnp.transpose(picker.astype(jnp.float32))
    for a in range(kerns):
        weights = lax.dot_general(
            picker,
            mixing[a],
            (((1,), (1,)), ((), ())),
            precision=lax.Precision.HIGHEST,
            preferred_element_type=jnp.float32,
        )
        for b in range(kerns):
            blend[a, b] = packed(jnp.broadcast_to(weights[:, b : b + 1], (part, cols)))

    for place in range(SLOTS):
        send_coeffs(0, 1, place)

    def collect(turn, half, finish=None):
        buffer = arrived[turn][half]
        pltpu.make_async_copy(buffer, buffer, recv_sem.at[turn, half]).wait()
        upper, lower = pairs(jnp.concatenate([buffer[place] for place in places], axis=0))
        for at, value in enumerate((upper, lower, upper, lower)):
            arrived_pair[pl.ds(at * depth, depth)] = value
        if finish is None:
            total[half] += dot(left[...], arrived_pair[...])
            return
        for step in range(2):
            at = pl.ds(step * rows // 2, rows // 2)
            finish(at, total[half, at] + dot(left[at], arrived_pair[...]))

    turns = tuple(sorted(range(1, kerns), key=lambda ahead: -min(ahead, kerns - ahead)))

    rest = part // 2 // PIECES

    def wait_fields(way, half, piece):
        size = gathered.at[half, pl.ds(1, kerns - 1), pl.ds(piece * rest, rest)]
        pltpu.make_async_copy(size, size, field_recv.at[way, half, piece]).wait()

    def send_field(way, half, ahead, piece):
        at = pl.ds(piece * rest, rest)
        copy = pltpu.make_async_remote_copy(
            src_ref=mixed_out.at[half, ahead, at] if way else fields.at[half, ahead, at],
            dst_ref=second.at[half, group, at] if way else gathered.at[half, kerns - ahead, at],
            send_sem=field_send.at[way],
            recv_sem=field_recv.at[way, half, piece],
            device_id=(kern_of(ahead), me),
            device_id_type=MESH,
        )
        copy.start()

    def send_first(half):
        for ahead in turns + (0,):
            at = pl.ds(pl.multiple_of(kern_of(ahead) * part, part), part)
            fields[half, ahead] = packed(doubled(total[half, at]))
        for piece in range(PIECES):
            for ahead in turns:
                send_field(0, half, ahead, piece)

    def mix(half):
        for piece in range(PIECES):
            at = pl.ds(piece * rest, rest)
            wait_fields(0, half, piece)
            for ahead in turns + (0,):
                value = blend[kern_of(ahead), group, at] * fields[half, 0, at]
                for other in range(1, kerns):
                    value += blend[kern_of(ahead), kern_of(other), at] * gathered[half, other, at]
                if ahead:
                    mixed_out[half, ahead, at] = value
                else:
                    second[half, group, at] = value
            for ahead in turns:
                send_field(1, half, ahead, piece)

    def spread(half, after_second=None):
        for piece in range(PIECES):
            wait_fields(1, half, piece)
        for quarter in range(kerns):
            upper, lower = pairs(second[half, quarter])
            set_pair(quarter * part, half, upper)
            set_pair(quarter * part + part // 2, half, lower)
        for step, (first, end) in enumerate(BLOCKS):
            result = dot(right[pl.ds(first * rank_max, (end - first) * rank_max)], pair[:, lanes(half)])
            keep_coeffs(1, half, first, result)
            for place in range(first, end):
                send_coeffs(1, half, place)
            if step == 1 and after_second is not None:
                after_second()

    collect(0, 0)
    send_first(0)
    mix(0)
    collect(0, 1)
    send_first(1)
    spread(0, lambda: mix(1))
    spread(1)
    diag_part()
    collect(1, 0)
    for step in range(kerns):
        at = pl.ds(step * part, part)
        total[0, at] = doubled(total[0, at])

    def finish(at, value):
        out_ref[at] = jnp.where(left_lanes(value), total[0, at], doubled(value))

    collect(1, 1, finish)
    pltpu.make_async_copy(coeffs, coeffs, send_sem).wait()
    for way, ref in enumerate((fields, mixed_out)):
        size = ref.at[:, pl.ds(1, kerns - 1)]
        pltpu.make_async_copy(size, size, field_send.at[way]).wait()


def local(tiles, kerns, *args):
    diag, left, right, offsets, ranks, mixing, index, rhs = args
    rows, cols = rhs.shape[1:]
    count, rank_max = left.shape[2:4]
    part = rows // kerns
    index = index.reshape(kerns, part)
    mixing = mixing.transpose(1, 2, 0)
    depth = count * rank_max // 2
    operands = (diag, left, right, offsets, ranks, mixing, index, rhs)
    operands = [pltpu.with_memory_space_constraint(value, pltpu.HBM) for value in operands]
    f32, bf16 = jnp.float32, jnp.bfloat16
    vmem = pltpu.VMEM
    return pl.pallas_call(
        functools.partial(kernel, tiles, kerns),
        out_shape=jax.ShapeDtypeStruct((rows, cols), f32),
        in_specs=[pl.BlockSpec(memory_space=pl.ANY)] * 8,
        out_specs=pl.BlockSpec(memory_space=pltpu.VMEM),
        scratch_shapes=[
            vmem((rows, cols), f32),
            vmem((rows, rows), f32),
            vmem((count, rank_max, rows), f32),
            vmem((SLOTS, rank_max, rows), f32),
            pltpu.SMEM(offsets.shape, jnp.int32),
            pltpu.SMEM(ranks.shape, jnp.int32),
            vmem(mixing.shape, f32),
            vmem(index.shape, jnp.int32),
            vmem((rows, 2 * rows), bf16),
            vmem((SLOTS * rank_max, 2 * rows), bf16),
            vmem((rows, 4 * depth), bf16),
            vmem((2 * rows, HALVES * cols), bf16),
            vmem((4 * depth, cols), bf16),
            vmem((2, HALVES, SLOTS, rank_max // 2, cols), f32),
            vmem((SLOTS, rank_max // 2, cols), f32),
            vmem((SLOTS, rank_max // 2, cols), f32),
            vmem((SLOTS, rank_max // 2, cols), f32),
            vmem((SLOTS, rank_max // 2, cols), f32),
            vmem((HALVES, rows, cols), f32),
            vmem((kerns, kerns, part // 2, cols), f32),
            vmem((HALVES, kerns, part // 2, cols), f32),
            vmem((HALVES, kerns, part // 2, cols), f32),
            vmem((HALVES, kerns, part // 2, cols), f32),
            vmem((HALVES, kerns, part // 2, cols), f32),
            pltpu.SemaphoreType.DMA((7,)),
            pltpu.SemaphoreType.DMA((len(BLOCKS),)),
            pltpu.SemaphoreType.DMA,
            pltpu.SemaphoreType.DMA((2, HALVES)),
            pltpu.SemaphoreType.DMA((2,)),
            pltpu.SemaphoreType.DMA((2, HALVES, PIECES)),
        ],
        compiler_params=pltpu.CompilerParams(collective_id=0, has_side_effects=True, vmem_limit_bytes=24 * 2**20),
    )(*operands)[None]


def solution(mesh):
    in_specs = (
        P("kern", "tile", None, None),
        P("kern", "tile", None, None, None),
        P("kern", "tile", None, None, None),
        P("kern", "tile", None),
        P("kern", "tile", None),
        P(),
        P("tile"),
        P("kern", "tile", None),
    )
    out_specs = P("kern", "tile", None)
    step = functools.partial(local, mesh.shape["tile"], mesh.shape["kern"])
    return jax.shard_map(step, mesh=mesh, in_specs=in_specs, out_specs=out_specs, check_vma=False)
```
